32 devices in a mesh: days: 2 (over y), chan: 4 (over z), tm: 2 (over x), freq: 2 (over core).
Axes of the slice: x: 2, y: 2, z: 4, core: 2. Of those that a mesh axis runs over, the one named last changes fastest.
Arguments:
- recording: bfloat16 [2048, 2048], P(('days', 'chan', 'freq'), 'tm'), parts along dimension 0, may hold values from -6 to 6
- trailing: bfloat16 [2048, 1024], P(('days', 'chan', 'freq')), parts along dimension 0, may hold values from -6 to 6
- whiten_filter: bfloat16 [1024, 64], P(('chan', 'freq')), may hold values from -0.75 to 0.75
- pair_list: int32 [8, 4], P(('days', 'chan')), parts along dimension 0, may hold values from -1 to 3, as said below
Outputs:
- cross_spectra: float32 [8, 4, 4, 2, 256, 256], P(('days', 'chan'), None, ('tm', 'freq')), parts along dimension 0
The draws below stay inside these ranges and needn't reach their ends.
There are 2 independent parts, one for each index of `days`. The reference program is written for one: setup_inputs(seed, part) draws one part's arguments, and reference() takes and returns one part's arrays. A program takes and returns all parts, laid end to end along the dimension named above; an argument that names none is the same for every part. Nothing has to cross between parts.
Inputs may be any that keep to these rules, and one draw needn't show every extreme that they name: `pair_list`: row a lists in its first slots distinct blocks b with |b - a| <= 3, then -1 in the remaining slots; every row lists at least one block, and some row of every draw fills all 4 slots.
All inputs are finite; a program needn't handle non-finite values.
Results may differ from the reference program's by a relative error of at most 0.0046.
Values may be sent and summed in bfloat16 or wider, within the bound.
A program may use at most 64 MiB of HBM per device.

```python
import math
import jax
import jax.numpy as jnp
from jax import lax

BLK = 256
WHIT = 64
WIN = 2048
FB = 512
REACH = 3
SLOTS = 4
HOP = 1024
NB = 4
CHANNELS = 1024
SEGS = 2
SAMPLES = 2048
BANDS = 4
BANDW = 128
N_CHAN = 4


def draw_pair_list(key, part):
    first_key = jax.random.fold_in(key, 11)
    second_key = jax.random.fold_in(key, 12)
    third_key = jax.random.fold_in(key, 13)
    fourth_key = jax.random.fold_in(key, 14)
    spread = 2 * REACH + 1
    owners = jnp.arange(NB, dtype=jnp.int32)[:, None]
    columns = jnp.arange(spread, dtype=jnp.int32)[None, :]
    candidates = owners + columns - REACH
    is_valid = (candidates >= 0) & (candidates < NB)
    scores = jax.random.randint(first_key, (NB, spread), 0, 65536, dtype=jnp.int32) * spread + columns
    scores = jnp.where(is_valid, scores, -1)
    ranking = jnp.argsort(-scores, axis=1, stable=True)
    picked = jnp.take_along_axis(candidates, ranking, axis=1)[:, :SLOTS]
    counts = jax.random.randint(second_key, (NB,), 1, 3, dtype=jnp.int32)
    is_heavy = jax.random.randint(third_key, (NB,), 0, 4, dtype=jnp.int32) == 0
    counts = jnp.where(is_heavy, SLOTS, counts)
    forced = jax.random.randint(fourth_key, (), 0, NB, dtype=jnp.int32)
    counts = jnp.where(jnp.arange(NB, dtype=jnp.int32) == forced, SLOTS, counts)
    counts = jnp.minimum(counts, SLOTS)
    slot_index = jnp.arange(SLOTS, dtype=jnp.int32)[None, :]
    return jnp.where(slot_index < counts[:, None], picked, -1).astype(jnp.int32)


def shard_levels(rng, extent, split, least, top_value):
    def one(dim, shards_of):
        steps = jax.random.uniform(jax.random.fold_in(jax.random.fold_in(rng, 6), dim), (shards_of,), jnp.float32, least / len(split), top_value / len(split))
        return jnp.repeat(jnp.exp(steps), extent[dim] // shards_of).reshape((-1,) + (1,) * (len(extent) - dim - 1))

    loudness = one(*split[0])
    for cut in split[1:]:
        loudness = loudness * one(*cut)
    return loudness


def bell_draw(rng, extent, scale, bound, cuts=(), kind=jnp.bfloat16):
    array = scale * jax.random.normal(rng, extent, jnp.float32)
    if cuts:
        array = array * shard_levels(rng, extent, cuts, -0.22, 0.18)
    return jnp.clip(array, -bound, bound).astype(kind)


def setup_inputs(seed: int = 0, part: int = 0) -> dict:
    seeds = jax.random.split(jax.random.key(seed), 5)
    part_keys = jax.random.split(jax.random.fold_in(seeds[4], part), 5)
    recording = bell_draw(part_keys[0], (CHANNELS, SAMPLES), 1.0, 6.0, ((0, 8), (1, 2)))
    trailing = bell_draw(part_keys[1], (CHANNELS, HOP), 1.0, 6.0, ((0, 8),))
    whiten_filter = bell_draw(seeds[2], (CHANNELS, WHIT), WHIT ** -0.5, 0.75, ((0, 8),))
    pair_list = draw_pair_list(jax.random.fold_in(jax.random.fold_in(seeds[4], part), 71), part)
    return dict(recording=recording, trailing=trailing, whiten_filter=whiten_filter, pair_list=pair_list)


def fourier_table(first_bin, bin_count, length):
    samples = jnp.arange(length, dtype=jnp.int32)[:, None]
    bin_index = first_bin + jnp.arange(bin_count, dtype=jnp.int32)[None, :]
    phase = samples * bin_index % length
    angle = 2.0 * math.pi / length * phase.astype(jnp.float32)
    taper = 0.5 - 0.5 * jnp.cos(2.0 * math.pi / length * jnp.arange(length, dtype=jnp.int32).astype(jnp.float32))
    normaliser = 1.0 / math.sqrt(0.375 * length)
    cosine = (taper[:, None] * jnp.cos(angle) * normaliser).astype(jnp.bfloat16)
    sine_table = (-taper[:, None] * jnp.sin(angle) * normaliser).astype(jnp.bfloat16)
    return (cosine, sine_table)

def reference(recording, trailing, whiten_filter, pair_list):
    signal = jnp.concatenate([recording, trailing], axis=1)
    channels = signal.shape[0]
    cosine, sine_table = fourier_table(0, FB, WIN)
    joined = jnp.concatenate([cosine, sine_table], axis=1).astype(jnp.float32)

    def transform(segment):
        start = (segment * HOP).astype(jnp.int32)
        pieces = lax.dynamic_slice_in_dim(signal, start, WIN, 1)
        return jnp.dot(pieces.astype(jnp.float32), joined).astype(jnp.bfloat16)
    raw = lax.map(transform, jnp.arange(SEGS, dtype=jnp.int32))
    raw = raw.transpose(1, 0, 2).reshape(channels, SEGS * 2 * FB)
    rim_width = WHIT // 2
    padded = jnp.pad(raw, ((rim_width, rim_width), (0, 0)))
    offset = jnp.arange(BLK + WHIT, dtype=jnp.int32)[None, :] - jnp.arange(BLK, dtype=jnp.int32)[:, None]
    inside = (offset >= 0) & (offset < WHIT)
    clipped = jnp.clip(offset, 0, WHIT - 1)

    def whiten_block(index):
        start = (index * BLK).astype(jnp.int32)
        window_rows = lax.dynamic_slice_in_dim(padded, start, BLK + WHIT, 0)
        weight_rows = lax.dynamic_slice_in_dim(whiten_filter, start, BLK, 0)
        band_matrix = jnp.where(inside, jnp.take_along_axis(weight_rows, clipped, axis=1), jnp.zeros((), weight_rows.dtype))
        predicted = jnp.dot(band_matrix.astype(jnp.float32), window_rows.astype(jnp.float32))
        own_rows = lax.dynamic_slice_in_dim(raw, start, BLK, 0)
        return (own_rows.astype(jnp.float32) - predicted).astype(jnp.bfloat16)
    spectra = lax.map(whiten_block, jnp.arange(N_CHAN, dtype=jnp.int32))
    arranged = spectra.reshape(NB, BLK, SEGS, 2, BANDS, BANDW).transpose(0, 3, 4, 1, 2, 5)
    arranged = arranged.reshape(NB, 2, BANDS, BLK, SEGS * BANDW)
    scaling = 1.0 / math.sqrt(SEGS * BANDW)

    def owner(owner_index):
        own_block = lax.dynamic_index_in_dim(arranged, owner_index, 0, keepdims=False).astype(jnp.float32)

        def one_slot(partner_index):
            partner = lax.dynamic_index_in_dim(arranged, jnp.maximum(partner_index, 0), 0, keepdims=False).astype(jnp.float32)
            real_part = jnp.einsum('gik,gjk->gij', own_block[0], partner[0]) + jnp.einsum('gik,gjk->gij', own_block[1], partner[1])
            imag_part = jnp.einsum('gik,gjk->gij', own_block[1], partner[0]) - jnp.einsum('gik,gjk->gij', own_block[0], partner[1])
            crossed = jnp.stack([real_part, imag_part], axis=1) * scaling
            return jnp.where(partner_index >= 0, crossed, jnp.zeros((), crossed.dtype))
        return lax.map(one_slot, lax.dynamic_index_in_dim(pair_list, owner_index, 0, keepdims=False))
    return lax.map(owner, jnp.arange(NB, dtype=jnp.int32))
```

```python
import functools
import math

import jax
import jax.numpy as jnp
from jax import lax
from jax.experimental import pallas as pl
from jax.experimental.pallas import tpu as pltpu
from jax.sharding import PartitionSpec as P

FB = 512
REACH = 3
SLOTS = 4


def shifted(block, axis, distance):
    devices = range(lax.axis_size(axis))
    route = [(i - distance, i) for i in devices if i - distance in devices]
    return lax.ppermute(block, axis, route)


def extended(value, sides, width):
    for axis, dim in sides:
        size, length = (lax.axis_size(axis), value.shape[dim])
        up = [(i, (i + 1) % size) for i in range(size - 1)]
        down = [(j, i) for i, j in up]
        last = lax.slice_in_dim(value, length - width, length, axis=dim)
        initial = lax.slice_in_dim(value, 0, width, axis=dim)
        before = lax.ppermute(last, axis, up)
        after = lax.ppermute(initial, axis, down)
        value = jnp.concatenate([before, value, after], axis=dim)
    return value


def fourier_table(first_bin, bin_count, length):
    samples = jnp.arange(length, dtype=jnp.int32)[:, None]
    bin_index = first_bin + jnp.arange(bin_count, dtype=jnp.int32)[None, :]
    phase = samples * bin_index % length
    angle = 2.0 * math.pi / length * phase.astype(jnp.float32)
    taper = 0.5 - 0.5 * jnp.cos(
        2.0 * math.pi / length * jnp.arange(length, dtype=jnp.int32).astype(jnp.float32)
    )
    normaliser = 1.0 / math.sqrt(0.375 * length)
    cosine = (taper[:, None] * jnp.cos(angle) * normaliser).astype(jnp.bfloat16)
    sine_table = (-taper[:, None] * jnp.sin(angle) * normaliser).astype(jnp.bfloat16)
    return (cosine, sine_table)


def general(recording, trailing, whiten_filter, pair_list):
    local_rows, local_span = recording.shape
    hop_size = trailing.shape[1]
    window_size = 2 * hop_size
    segment_count = local_span // hop_size
    following = shifted(recording, "tm", -1)
    is_last = lax.axis_index("tm") == lax.axis_size("tm") - 1
    following = jnp.where(is_last, trailing, following)
    signal = jnp.concatenate([recording, following], axis=1)
    segments = jnp.stack([signal], axis=1)
    stacked_segments = segments.reshape(local_rows * segment_count, window_size)
    bin_step = min(256, FB)
    real_bins = []
    imag_bins = []
    for first_bin in range(0, FB, bin_step):
        cosine, sine_table = fourier_table(first_bin, bin_step, window_size)
        joined = jnp.concatenate([cosine, sine_table], axis=1)
        product = jnp.dot(stacked_segments, joined, preferred_element_type=jnp.float32).astype(
            jnp.bfloat16
        )
        real_bins.append(product[:, :bin_step])
        imag_bins.append(product[:, bin_step:])
    real_spec = jnp.concatenate(real_bins, axis=1)
    imag_spec = jnp.concatenate(imag_bins, axis=1)
    raw_spectra = jnp.stack([real_spec, imag_spec])
    tap_count = whiten_filter.shape[1]
    rim_width = tap_count // 2
    reach_rows = local_rows + tap_count
    skewed = jnp.pad(whiten_filter, ((0, 0), (0, local_rows + 1))).reshape(-1)
    band_matrix = skewed[: local_rows * reach_rows].reshape(local_rows, reach_rows)
    padded = extended(raw_spectra, ((("chan", "freq"), 1),), rim_width)
    predicted = jnp.einsum("ij,ajk->aik", band_matrix, padded, preferred_element_type=jnp.float32)
    whitened = (raw_spectra.astype(jnp.float32) - predicted).astype(jnp.bfloat16)
    spectra = whitened.reshape(2, local_rows, segment_count, FB)
    tm_count = lax.axis_size("tm")
    freq_count = lax.axis_size("freq")
    pieces = lax.all_to_all(spectra[None], ("tm", "freq"), split_axis=4, concat_axis=0, tiled=True)
    band_width = pieces.shape[-1]
    pieces = pieces.reshape(tm_count, freq_count, 2, local_rows, segment_count, band_width)
    banded = pieces.transpose(2, 1, 3, 0, 4, 5).reshape(
        2, freq_count * local_rows, tm_count * segment_count, band_width
    )
    block_rows = banded.shape[1]
    own_block = banded.reshape(2, block_rows, -1)
    depth = own_block.shape[2]
    scaling = 1.0 / math.sqrt(depth)
    block_index = lax.axis_index("chan")
    slot_list = pair_list[0]
    nearby = []
    for distance in range(-REACH, REACH + 1):
        if distance == 0:
            nearby.append(own_block)
        else:
            nearby.append(shifted(own_block, "chan", -distance))
    stacked = jnp.stack(nearby)

    def fetch_partner(partner_index):
        return lax.dynamic_index_in_dim(
            stacked, partner_index - block_index + REACH, 0, keepdims=False
        )

    left_side = jnp.concatenate([own_block[0], own_block[1]], axis=1)
    flipped = jnp.concatenate([own_block[1], -own_block[0]], axis=1)
    contract = (((1,), (1,)), ((), ()))

    def one_slot(partner_index):
        partner = fetch_partner(partner_index)
        right_side = jnp.concatenate([partner[0], partner[1]], axis=1)
        real_part = (
            lax.dot_general(left_side, right_side, contract, preferred_element_type=jnp.float32)
            * scaling
        )
        imag_part = (
            lax.dot_general(flipped, right_side, contract, preferred_element_type=jnp.float32)
            * scaling
        )
        crossed = jnp.stack([real_part, imag_part])
        return jnp.where(partner_index >= 0, crossed, jnp.zeros((), jnp.float32))

    result = jnp.stack([one_slot(slot_list[slot_index]) for slot_index in range(SLOTS)])
    return result.reshape(1, SLOTS, 1, 2, block_rows, block_rows)


MESH = pl.DeviceIdType.MESH
TIERS = ((64, 128), (0, 64), (192, 64))
PIECES = 4
STEP = 32
TILE = 64


def spectra_kernel(
    chan_count,
    window_slots,
    rec_ref,
    trail_ref,
    filt_ref,
    gathered,
    samples,
    filters,
    table,
    coarse,
    raw,
    span_sems,
    core_sems,
    pass_sems,
    rim_sems,
    block_sems,
):
    me = lax.axis_index("chan")
    tm = lax.axis_index("tm")
    core = lax.axis_index("freq")
    rows, hop = rec_ref.shape
    window = 2 * hop
    width = table.shape[1] // 2
    block_rows = 2 * rows
    rim = filt_ref.shape[1] // 2
    has_left = me > 0
    has_right = me < chan_count - 1
    other_tm = {"tm": 1 - tm}
    other_core = {"freq": 1 - core}
    left = {"chan": me - 1}
    right = {"chan": me + 1}

    def remote(source, target, sems, index, device):
        return pltpu.make_async_remote_copy(
            src_ref=source,
            dst_ref=target,
            send_sem=sems.at[(0,) + index],
            recv_sem=sems.at[(1,) + index],
            device_id=device,
            device_id_type=MESH,
        )

    barrier = pltpu.get_barrier_semaphore()
    pl.semaphore_signal(barrier, inc=1, device_id=other_tm, device_id_type=MESH)
    pl.semaphore_signal(barrier, inc=1, device_id=other_core, device_id_type=MESH)

    @pl.when(has_left)
    def _():
        pl.semaphore_signal(barrier, inc=1, device_id=left, device_id_type=MESH)

    @pl.when(has_right)
    def _():
        pl.semaphore_signal(barrier, inc=1, device_id=right, device_id_type=MESH)

    pl.semaphore_wait(barrier, 2 + has_left.astype(jnp.int32) + has_right.astype(jnp.int32))

    piece = rows // PIECES

    def piece_rows(index):
        return pl.ds(index * piece, piece)

    span_copies = [
        remote(
            rec_ref.at[piece_rows(p)],
            samples.at[tm, core, piece_rows(p)],
            span_sems,
            (p,),
            other_tm,
        )
        for p in range(PIECES)
    ]
    for copy in span_copies:
        copy.start()
    core_copies = [
        remote(rec_ref, samples.at[tm, core], core_sems, (0,), other_core),
        remote(trail_ref, samples.at[2, core], core_sems, (1,), other_core),
        remote(filt_ref, filters.at[core], core_sems, (2,), other_core),
    ]
    for copy in core_copies:
        copy.start()

    samples[tm, core] = rec_ref[...]
    samples[2, core] = trail_ref[...]
    filters[core] = filt_ref[...]

    first_bin = (tm * 2 + core) * width
    unit = 2.0 * math.pi / window
    bins = first_bin + lax.broadcasted_iota(jnp.int32, (1, width), 1)

    def angles(count, scale, factor):
        steps = scale * lax.broadcasted_iota(jnp.int32, (count, width), 0)
        return unit * jnp.bitwise_and(steps * factor, window - 1).astype(jnp.float32)

    parts = window // STEP
    coarse_angle = angles(parts, STEP, bins)
    coarse_turn = angles(parts, STEP, 1)
    coarse[0] = jnp.cos(coarse_angle)
    coarse[1] = jnp.sin(coarse_angle)
    coarse[2] = jnp.cos(coarse_turn)
    coarse[3] = jnp.sin(coarse_turn)
    fine_angle = angles(STEP, 1, bins)
    fine_turn = angles(STEP, 1, 1)
    fine_cos, fine_sin = jnp.cos(fine_angle), jnp.sin(fine_angle)
    turn_cos, turn_sin = jnp.cos(fine_turn), jnp.sin(fine_turn)
    normaliser = 1.0 / math.sqrt(0.375 * window)

    def fill(part, carry):
        c, s, tc, ts = (coarse[k, pl.ds(part, 1), :] for k in range(4))
        taper = (0.5 - 0.5 * (tc * turn_cos - ts * turn_sin)) * normaliser
        at = pl.ds(pl.multiple_of(part * STEP, STEP), STEP)
        table[at, :width] = (taper * (c * fine_cos - s * fine_sin)).astype(jnp.bfloat16)
        table[at, width:] = (-taper * (s * fine_cos + c * fine_sin)).astype(jnp.bfloat16)
        return carry

    lax.fori_loop(0, parts, fill, 0)

    @pl.when(jnp.logical_not(has_left))
    def _():
        raw[0:rim] = jnp.zeros((rim, raw.shape[1]), raw.dtype)

    @pl.when(jnp.logical_not(has_right))
    def _():
        raw[rim + block_rows : 2 * rim + block_rows] = jnp.zeros((rim, raw.shape[1]), raw.dtype)

    pass_copies = [
        remote(
            samples.at[1 - tm, core, piece_rows(p)],
            samples.at[1 - tm, core, piece_rows(p)],
            pass_sems,
            (p,),
            other_core,
        )
        for p in range(PIECES)
    ]
    arriving = [
        remote(
            rec_ref.at[piece_rows(p)],
            samples.at[1 - tm, core, piece_rows(p)],
            span_sems,
            (p,),
            other_tm,
        )
        for p in range(PIECES)
    ]
    for p in range(PIECES):
        arriving[p].wait_recv()
        pass_copies[p].start()

    def transform(half):
        pair = samples[0:2, half].reshape(2 * rows, hop)
        later = samples[1:3, half].reshape(2 * rows, hop)
        product = jnp.dot(pair, table[:hop], preferred_element_type=jnp.float32) + jnp.dot(
            later, table[hop:], preferred_element_type=jnp.float32
        )
        product = product.astype(jnp.bfloat16)
        at = pl.ds(pl.multiple_of(rim + half * rows, rim), rows)
        raw[at, 0:width] = product[:rows, :width]
        raw[at, width : 2 * width] = product[rows:, :width]
        raw[at, 2 * width : 3 * width] = product[:rows, width:]
        raw[at, 3 * width : 4 * width] = product[rows:, width:]

    transform(core)
    other = 1 - core
    remote(rec_ref, samples.at[tm, other], core_sems, (0,), other_core).wait_recv()
    remote(trail_ref, samples.at[2, other], core_sems, (1,), other_core).wait_recv()
    remote(filt_ref, filters.at[other], core_sems, (2,), other_core).wait_recv()
    for p in range(PIECES):
        remote(
            samples.at[1 - tm, core, piece_rows(p)],
            samples.at[1 - tm, other, piece_rows(p)],
            pass_sems,
            (p,),
            other_core,
        ).wait_recv()
    transform(other)

    to_right = remote(raw.at[block_rows : block_rows + rim], raw.at[0:rim], rim_sems, (0,), right)
    to_left = remote(
        raw.at[rim : 2 * rim],
        raw.at[rim + block_rows : 2 * rim + block_rows],
        rim_sems,
        (1,),
        left,
    )

    @pl.when(has_right)
    def _():
        to_right.start()

    @pl.when(has_left)
    def _():
        to_left.start()

    own_slot = lax.rem(me, window_slots)

    def whiten(tile):
        weights = filters[tile * TILE // rows, tile * TILE % rows : tile * TILE % rows + TILE]
        wide = jnp.concatenate(
            [weights.astype(jnp.float32), jnp.zeros((TILE, TILE), jnp.float32)], axis=1
        )
        band = pltpu.roll(wide, 0, 1, stride=1, stride_axis=0).astype(jnp.bfloat16)
        near = raw[tile * TILE : tile * TILE + 2 * TILE]
        predicted = jnp.dot(band, near, preferred_element_type=jnp.float32)
        mine = raw[rim + tile * TILE : rim + tile * TILE + TILE].astype(jnp.float32)
        gathered[own_slot, tile * TILE : tile * TILE + TILE] = (mine - predicted).astype(
            jnp.bfloat16
        )

    def block_copy(direction, distance, tier):
        start, count = TIERS[tier]
        source = me - distance if direction == 0 else me + distance
        slot = lax.rem(jnp.clip(source, 0, chan_count - 1), window_slots)
        at = gathered.at[slot, pl.ds(start, count)]
        return remote(
            at, at, block_sems, (direction, distance, tier), right if direction == 0 else left
        )

    def landed(direction, distance, tier):
        start, count = TIERS[tier]
        source = me - distance if direction == 0 else me + distance
        slot = lax.rem(jnp.clip(source, 0, chan_count - 1), window_slots)
        at = gathered.at[slot, pl.ds(start, count)]
        return remote(
            at, at, block_sems, (direction, distance - 1, tier), right if direction == 0 else left
        )

    ahead = (has_right, has_left)

    def send_own(tier):
        for direction in range(2):

            @pl.when(ahead[direction])
            def _():
                block_copy(direction, 0, tier).start()

    whiten(1)
    whiten(2)
    send_own(0)

    @pl.when(has_left)
    def _():
        remote(raw.at[0:rim], raw.at[0:rim], rim_sems, (0,), right).wait_recv()

    whiten(0)
    send_own(1)

    @pl.when(has_right)
    def _():
        at = raw.at[rim + block_rows : 2 * rim + block_rows]
        remote(at, at, rim_sems, (1,), left).wait_recv()

    whiten(3)
    send_own(2)

    furthest = min(REACH, chan_count - 1)

    def exists(direction, distance):
        return me - distance >= 0 if direction == 0 else me + distance < chan_count

    for distance in range(1, furthest + 1):
        for tier in range(len(TIERS)):
            for direction in range(2):

                @pl.when(exists(direction, distance))
                def _():
                    landed(direction, distance, tier).wait_recv()

                if distance < furthest:

                    @pl.when(jnp.logical_and(exists(direction, distance), ahead[direction]))
                    def _():
                        block_copy(direction, distance, tier).start()

    for copy in span_copies + core_copies + pass_copies:
        copy.wait_send()

    @pl.when(has_right)
    def _():
        to_right.wait_send()

    @pl.when(has_left)
    def _():
        to_left.wait_send()

    for distance in range(furthest):
        for tier in range(len(TIERS)):
            for direction in range(2):

                @pl.when(jnp.logical_and(exists(direction, distance), ahead[direction]))
                def _():
                    block_copy(direction, distance, tier).wait_send()


def cross_kernel(window_slots, scaling, pairs_ref, gathered, out_ref):
    slot = pl.program_id(0)
    me = lax.rem(lax.axis_index("chan"), window_slots)
    partner = pairs_ref[0, slot]
    half = gathered.shape[2] // 2
    contract = (((1,), (1,)), ((), ()))

    @pl.when(partner >= 0)
    def _():
        own = gathered[me]
        right_side = gathered[lax.rem(jnp.maximum(partner, 0), window_slots)]
        turned = jnp.concatenate([own[:, half:], -own[:, :half]], axis=1)
        real = lax.dot_general(own, right_side, contract, preferred_element_type=jnp.float32)
        out_ref[0, 0, 0, 0] = real * scaling
        imag = lax.dot_general(turned, right_side, contract, preferred_element_type=jnp.float32)
        out_ref[0, 0, 0, 1] = imag * scaling

    @pl.when(partner < 0)
    def _():
        out_ref[...] = jnp.zeros_like(out_ref)


def fused(recording, trailing, whiten_filter, pair_list):
    rows, hop = recording.shape
    chan_count = lax.axis_size("chan")
    window_slots = min(chan_count, 2 * REACH + 1)
    taps = whiten_filter.shape[1]
    width = FB // (lax.axis_size("tm") * lax.axis_size("freq"))
    block_rows = 2 * rows
    depth = 2 * width
    furthest = min(REACH, chan_count - 1)
    vmem = pl.BlockSpec(memory_space=pltpu.VMEM)
    gathered = pl.pallas_call(
        functools.partial(spectra_kernel, chan_count, window_slots),
        out_shape=jax.ShapeDtypeStruct((window_slots, block_rows, 2 * depth), jnp.bfloat16),
        in_specs=[vmem] * 3,
        out_specs=vmem,
        scratch_shapes=[
            pltpu.VMEM((3, 2, rows, hop), jnp.bfloat16),
            pltpu.VMEM((2, rows, taps), jnp.bfloat16),
            pltpu.VMEM((2 * hop, 2 * width), jnp.bfloat16),
            pltpu.VMEM((4, 2 * hop // STEP, width), jnp.float32),
            pltpu.VMEM((block_rows + taps, 2 * depth), jnp.bfloat16),
            pltpu.SemaphoreType.DMA((2, PIECES)),
            pltpu.SemaphoreType.DMA((2, 3)),
            pltpu.SemaphoreType.DMA((2, PIECES)),
            pltpu.SemaphoreType.DMA((2, 2)),
            pltpu.SemaphoreType.DMA((2, 2, furthest, len(TIERS))),
        ],
        compiler_params=pltpu.CompilerParams(collective_id=0, has_side_effects=True),
    )(recording, trailing, whiten_filter)
    return pl.pallas_call(
        functools.partial(cross_kernel, window_slots, 1.0 / math.sqrt(depth)),
        out_shape=jax.ShapeDtypeStruct((1, SLOTS, 1, 2, block_rows, block_rows), jnp.float32),
        grid_spec=pltpu.PrefetchScalarGridSpec(
            num_scalar_prefetch=1,
            grid=(SLOTS,),
            in_specs=[vmem],
            out_specs=pl.BlockSpec(
                (1, 1, 1, 2, block_rows, block_rows), lambda slot, pairs: (0, slot, 0, 0, 0, 0)
            ),
        ),
    )(pair_list, gathered)


def local(recording, trailing, whiten_filter, pair_list):
    shapes = (recording.shape, trailing.shape, whiten_filter.shape)
    counts = (lax.axis_size("tm"), lax.axis_size("freq"))
    if shapes == ((128, 1024), (128, 1024), (128, 64)) and counts == (2, 2):
        return fused(recording, trailing, whiten_filter, pair_list)
    return general(recording, trailing, whiten_filter, pair_list)


def solution(mesh):
    placed = (
        P(("days", "chan", "freq"), "tm"),
        P(("days", "chan", "freq"), None),
        P(("chan", "freq"), None),
        P(("days", "chan"), None),
    )
    return jax.shard_map(
        local,
        mesh=mesh,
        in_specs=placed,
        out_specs=P(("days", "chan"), None, ("tm", "freq"), None, None, None),
        check_vma=False,
    )
```

```python
import functools
import math

import jax
import jax.numpy as jnp
from jax import lax
from jax.experimental import pallas as pl
from jax.experimental.pallas import tpu as pltpu
from jax.sharding import PartitionSpec as P

FB = 512
REACH = 3
SLOTS = 4


def shifted(block, axis, distance):
    devices = range(lax.axis_size(axis))
    route = [(i - distance, i) for i in devices if i - distance in devices]
    return lax.ppermute(block, axis, route)


def extended(value, sides, width):
    for axis, dim in sides:
        size, length = (lax.axis_size(axis), value.shape[dim])
        up = [(i, (i + 1) % size) for i in range(size - 1)]
        down = [(j, i) for i, j in up]
        last = lax.slice_in_dim(value, length - width, length, axis=dim)
        initial = lax.slice_in_dim(value, 0, width, axis=dim)
        before = lax.ppermute(last, axis, up)
        after = lax.ppermute(initial, axis, down)
        value = jnp.concatenate([before, value, after], axis=dim)
    return value


def fourier_table(first_bin, bin_count, length):
    samples = jnp.arange(length, dtype=jnp.int32)[:, None]
    bin_index = first_bin + jnp.arange(bin_count, dtype=jnp.int32)[None, :]
    phase = samples * bin_index % length
    angle = 2.0 * math.pi / length * phase.astype(jnp.float32)
    taper = 0.5 - 0.5 * jnp.cos(
        2.0 * math.pi / length * jnp.arange(length, dtype=jnp.int32).astype(jnp.float32)
    )
    normaliser = 1.0 / math.sqrt(0.375 * length)
    cosine = (taper[:, None] * jnp.cos(angle) * normaliser).astype(jnp.bfloat16)
    sine_table = (-taper[:, None] * jnp.sin(angle) * normaliser).astype(jnp.bfloat16)
    return (cosine, sine_table)


def general(recording, trailing, whiten_filter, pair_list):
    local_rows, local_span = recording.shape
    hop_size = trailing.shape[1]
    window_size = 2 * hop_size
    segment_count = local_span // hop_size
    following = shifted(recording, "tm", -1)
    is_last = lax.axis_index("tm") == lax.axis_size("tm") - 1
    following = jnp.where(is_last, trailing, following)
    signal = jnp.concatenate([recording, following], axis=1)
    segments = jnp.stack([signal], axis=1)
    stacked_segments = segments.reshape(local_rows * segment_count, window_size)
    bin_step = min(256, FB)
    real_bins = []
    imag_bins = []
    for first_bin in range(0, FB, bin_step):
        cosine, sine_table = fourier_table(first_bin, bin_step, window_size)
        joined = jnp.concatenate([cosine, sine_table], axis=1)
        product = jnp.dot(stacked_segments, joined, preferred_element_type=jnp.float32).astype(
            jnp.bfloat16
        )
        real_bins.append(product[:, :bin_step])
        imag_bins.append(product[:, bin_step:])
    real_spec = jnp.concatenate(real_bins, axis=1)
    imag_spec = jnp.concatenate(imag_bins, axis=1)
    raw_spectra = jnp.stack([real_spec, imag_spec])
    tap_count = whiten_filter.shape[1]
    rim_width = tap_count // 2
    reach_rows = local_rows + tap_count
    skewed = jnp.pad(whiten_filter, ((0, 0), (0, local_rows + 1))).reshape(-1)
    band_matrix = skewed[: local_rows * reach_rows].reshape(local_rows, reach_rows)
    padded = extended(raw_spectra, ((("chan", "freq"), 1),), rim_width)
    predicted = jnp.einsum("ij,ajk->aik", band_matrix, padded, preferred_element_type=jnp.float32)
    whitened = (raw_spectra.astype(jnp.float32) - predicted).astype(jnp.bfloat16)
    spectra = whitened.reshape(2, local_rows, segment_count, FB)
    tm_count = lax.axis_size("tm")
    freq_count = lax.axis_size("freq")
    pieces = lax.all_to_all(spectra[None], ("tm", "freq"), split_axis=4, concat_axis=0, tiled=True)
    band_width = pieces.shape[-1]
    pieces = pieces.reshape(tm_count, freq_count, 2, local_rows, segment_count, band_width)
    banded = pieces.transpose(2, 1, 3, 0, 4, 5).reshape(
        2, freq_count * local_rows, tm_count * segment_count, band_width
    )
    block_rows = banded.shape[1]
    own_block = banded.reshape(2, block_rows, -1)
    depth = own_block.shape[2]
    scaling = 1.0 / math.sqrt(depth)
    block_index = lax.axis_index("chan")
    slot_list = pair_list[0]
    nearby = []
    for distance in range(-REACH, REACH + 1):
        if distance == 0:
            nearby.append(own_block)
        else:
            nearby.append(shifted(own_block, "chan", -distance))
    stacked = jnp.stack(nearby)

    def fetch_partner(partner_index):
        return lax.dynamic_index_in_dim(
            stacked, partner_index - block_index + REACH, 0, keepdims=False
        )

    left_side = jnp.concatenate([own_block[0], own_block[1]], axis=1)
    flipped = jnp.concatenate([own_block[1], -own_block[0]], axis=1)
    contract = (((1,), (1,)), ((), ()))

    def one_slot(partner_index):
        partner = fetch_partner(partner_index)
        right_side = jnp.concatenate([partner[0], partner[1]], axis=1)
        real_part = (
            lax.dot_general(left_side, right_side, contract, preferred_element_type=jnp.float32)
            * scaling
        )
        imag_part = (
            lax.dot_general(flipped, right_side, contract, preferred_element_type=jnp.float32)
            * scaling
        )
        crossed = jnp.stack([real_part, imag_part])
        return jnp.where(partner_index >= 0, crossed, jnp.zeros((), jnp.float32))

    result = jnp.stack([one_slot(slot_list[slot_index]) for slot_index in range(SLOTS)])
    return result.reshape(1, SLOTS, 1, 2, block_rows, block_rows)


MESH = pl.DeviceIdType.MESH
PIECES = 4
STEP = 32


def spectra_kernel(
    chan_count,
    window_slots,
    scaling,
    rec_ref,
    trail_ref,
    filt_ref,
    crossed,
    samples,
    filters,
    bands,
    table,
    coarse,
    raw,
    gathered,
    local_sems,
    span_sems,
    core_sems,
    pass_sems,
    rim_sems,
    block_sems,
):
    me = lax.axis_index("chan")
    tm = lax.axis_index("tm")
    core = lax.axis_index("freq")
    rows, hop = rec_ref.shape
    window = 2 * hop
    width = table.shape[1] // 2
    block_rows = 2 * rows
    taps = filt_ref.shape[0]
    rim = taps // 2
    piece = rows // PIECES
    has_left = me > 0
    has_right = me < chan_count - 1
    other = 1 - core
    other_tm = {"tm": 1 - tm}
    other_core = {"freq": 1 - core}
    left = {"chan": me - 1}
    right = {"chan": me + 1}

    def remote(source, target, sems, index, device):
        return pltpu.make_async_remote_copy(
            src_ref=source,
            dst_ref=target,
            send_sem=sems.at[(0,) + index],
            recv_sem=sems.at[(1,) + index],
            device_id=device,
            device_id_type=MESH,
        )

    def half(which):
        return pl.ds(pl.multiple_of(which * rows, rows), rows)

    barrier = pltpu.get_barrier_semaphore()
    pl.semaphore_signal(barrier, inc=1, device_id=other_tm, device_id_type=MESH)
    pl.semaphore_signal(barrier, inc=1, device_id=other_core, device_id_type=MESH)

    @pl.when(has_left)
    def _():
        pl.semaphore_signal(barrier, inc=1, device_id=left, device_id_type=MESH)

    @pl.when(has_right)
    def _():
        pl.semaphore_signal(barrier, inc=1, device_id=right, device_id_type=MESH)

    own_copies = [
        pltpu.make_async_copy(rec_ref, samples.at[tm, half(core)], local_sems.at[0]),
        pltpu.make_async_copy(trail_ref, samples.at[2, half(core)], local_sems.at[1]),
        pltpu.make_async_copy(filt_ref, filters.at[core], local_sems.at[2]),
    ]
    for copy in own_copies:
        copy.start()

    pl.semaphore_wait(barrier, 2 + has_left.astype(jnp.int32) + has_right.astype(jnp.int32))

    def piece_start(which, step):
        return pl.multiple_of(
            (1 - which) * (PIECES - 1 - step) * piece + which * step * piece, piece
        )

    def piece_in_block(which, step):
        start = which * rows + piece_start(which, step)
        return pl.ds(pl.multiple_of(start, piece), piece)

    span_copies = [
        remote(
            rec_ref.at[pl.ds(piece_start(core, p), piece)],
            samples.at[tm, piece_in_block(core, p)],
            span_sems,
            (p,),
            other_tm,
        )
        for p in range(PIECES)
    ]
    for copy in span_copies:
        copy.start()
    core_copies = [
        remote(rec_ref, samples.at[tm, half(core)], core_sems, (0,), other_core),
        remote(trail_ref, samples.at[2, half(core)], core_sems, (1,), other_core),
        remote(filt_ref, filters.at[core], core_sems, (2,), other_core),
    ]
    for copy in core_copies:
        copy.start()

    first_bin = (tm * 2 + core) * width
    unit = 2.0 * math.pi / window
    bins = first_bin + lax.broadcasted_iota(jnp.int32, (1, width), 1)

    def angles(count, scale, factor):
        steps = scale * lax.broadcasted_iota(jnp.int32, (count, width), 0)
        return unit * jnp.bitwise_and(steps * factor, window - 1).astype(jnp.float32)

    parts = window // STEP
    coarse_angle = angles(parts, STEP, bins)
    coarse_turn = angles(parts, STEP, 1)
    coarse[0] = jnp.cos(coarse_angle)
    coarse[1] = jnp.sin(coarse_angle)
    coarse[2] = jnp.cos(coarse_turn)
    coarse[3] = jnp.sin(coarse_turn)
    fine_angle = angles(STEP, 1, bins)
    fine_turn = angles(STEP, 1, 1)
    fine_cos, fine_sin = jnp.cos(fine_angle), jnp.sin(fine_angle)
    turn_cos, turn_sin = jnp.cos(fine_turn), jnp.sin(fine_turn)
    normaliser = 1.0 / math.sqrt(0.375 * window)

    def fill(part, carry):
        c, s, tc, ts = (coarse[k, pl.ds(part, 1), :] for k in range(4))
        taper = (0.5 - 0.5 * (tc * turn_cos - ts * turn_sin)) * normaliser
        at = pl.ds(pl.multiple_of(part * STEP, STEP), STEP)
        table[at, :width] = (taper * (c * fine_cos - s * fine_sin)).astype(jnp.bfloat16)
        table[at, width:] = (-taper * (s * fine_cos + c * fine_sin)).astype(jnp.bfloat16)
        return carry

    lax.fori_loop(0, parts, fill, 0)

    @pl.when(jnp.logical_not(has_left))
    def _():
        raw[0:rim] = jnp.zeros((rim, raw.shape[1]), raw.dtype)

    @pl.when(jnp.logical_not(has_right))
    def _():
        raw[rim + block_rows : 2 * rim + block_rows] = jnp.zeros((rim, raw.shape[1]), raw.dtype)

    for copy in own_copies:
        copy.wait()
    remote(filt_ref, filters.at[other], core_sems, (2,), other_core).wait_recv()
    for which in range(2):
        weights = jnp.transpose(filters[which].astype(jnp.float32))
        wide = jnp.concatenate([weights, jnp.zeros((rows, 128 - taps), jnp.float32)], axis=1)
        for p in range(PIECES):
            rolled = pltpu.roll(
                wide[p * piece : (p + 1) * piece], 0, 1, stride=1, stride_axis=0
            )
            bands[which * PIECES + p] = rolled.astype(jnp.bfloat16)

    remote(rec_ref, samples.at[tm, half(other)], core_sems, (0,), other_core).wait_recv()
    remote(trail_ref, samples.at[2, half(other)], core_sems, (1,), other_core).wait_recv()

    own_slot = lax.rem(me, window_slots)

    def whiten(tile):
        near = raw[tile * piece : tile * piece + piece + taps]
        predicted = jnp.dot(
            bands[tile][:, : piece + taps], near, preferred_element_type=jnp.float32
        )
        mine = raw[rim + tile * piece : rim + (tile + 1) * piece].astype(jnp.float32)
        gathered[own_slot, tile * piece : (tile + 1) * piece] = (mine - predicted).astype(
            jnp.bfloat16
        )

    tiers = [((PIECES - 1) * piece, 2 * piece)]
    for p in range(1, PIECES):
        tiers += [((PIECES - 1 - p) * piece, piece), ((PIECES + p) * piece, piece)]

    def block_copy(direction, distance, tier, sem):
        start, count = tiers[tier]
        source = me - distance if direction == 0 else me + distance
        slot = lax.rem(jnp.clip(source, 0, chan_count - 1), window_slots)
        at = gathered.at[slot, pl.ds(start, count)]
        return remote(at, at, block_sems, (direction, sem, tier), right if direction == 0 else left)

    def outgoing(direction, distance, tier):
        return block_copy(direction, distance, tier, distance)

    def landed(direction, distance, tier):
        return block_copy(direction, distance, tier, distance - 1)

    ahead = (has_right, has_left)

    def send_own(*chosen):
        for direction in range(2):

            @pl.when(ahead[direction])
            def _():
                for tier in chosen:
                    outgoing(direction, 0, tier).start()

    to_right = remote(raw.at[block_rows : block_rows + rim], raw.at[0:rim], rim_sems, (0,), right)
    to_left = remote(
        raw.at[rim : 2 * rim],
        raw.at[rim + block_rows : 2 * rim + block_rows],
        rim_sems,
        (1,),
        left,
    )
    pass_copies = []
    for p in range(PIECES):
        mine = samples.at[1 - tm, piece_in_block(core, p)]
        theirs = samples.at[1 - tm, piece_in_block(other, p)]
        remote(mine, mine, span_sems, (p,), other_tm).wait_recv()
        passing = remote(mine, mine, pass_sems, (p,), other_core)
        passing.start()
        pass_copies.append(passing)
        remote(theirs, theirs, pass_sems, (p,), other_core).wait_recv()

        low, high = (PIECES - 1 - p) * piece, (PIECES + p) * piece
        first = [samples[0:2, at : at + piece].reshape(2 * piece, hop) for at in (low, high)]
        second = [samples[1:3, at : at + piece].reshape(2 * piece, hop) for at in (low, high)]
        product = jnp.dot(
            jnp.concatenate(first, axis=0), table[:hop], preferred_element_type=jnp.float32
        ) + jnp.dot(
            jnp.concatenate(second, axis=0), table[hop:], preferred_element_type=jnp.float32
        )
        product = product.astype(jnp.bfloat16)
        for index, at in enumerate((low, high)):
            for segment in range(2):
                found = product[(2 * index + segment) * piece : (2 * index + segment + 1) * piece]
                where = pl.ds(rim + at, piece)
                raw[where, segment * width : (segment + 1) * width] = found[:, :width]
                raw[where, (2 + segment) * width : (3 + segment) * width] = found[:, width:]
        if p == PIECES - 1:

            @pl.when(has_right)
            def _():
                to_right.start()

            @pl.when(has_left)
            def _():
                to_left.start()

        if p > 0:
            whiten(PIECES - p)
            whiten(PIECES + p - 1)
            send_own(*((0,) if p == 1 else (2 * p - 3, 2 * p - 2)))

    furthest = min(REACH, chan_count - 1)

    def exists(direction, distance):
        return me - distance >= 0 if direction == 0 else me + distance < chan_count

    def advance(distance, chosen):
        for tier in chosen:
            for direction in range(2):

                @pl.when(exists(direction, distance))
                def _():
                    landed(direction, distance, tier).wait_recv()

                if distance < furthest:

                    @pl.when(jnp.logical_and(exists(direction, distance), ahead[direction]))
                    def _():
                        outgoing(direction, distance, tier).start()

    early = 3
    advance(1, range(early))

    @pl.when(has_left)
    def _():
        remote(raw.at[0:rim], raw.at[0:rim], rim_sems, (0,), right).wait_recv()

    whiten(0)
    send_own(2 * PIECES - 3)

    @pl.when(has_right)
    def _():
        at = raw.at[rim + block_rows : 2 * rim + block_rows]
        remote(at, at, rim_sems, (1,), left).wait_recv()

    whiten(2 * PIECES - 1)
    send_own(2 * PIECES - 2)

    @pl.when(has_right)
    def _():
        to_right.wait_send()

    @pl.when(has_left)
    def _():
        to_left.wait_send()

    own = gathered[own_slot]
    middle = own.shape[1] // 2
    raw[0:block_rows] = jnp.concatenate([own[:, middle:], -own[:, :middle]], axis=1)
    contract = (((1,), (1,)), ((), ()))

    def cross(slot):
        partner = gathered[slot]
        for part, side in enumerate((gathered[own_slot], raw[0:block_rows])):
            crossed[slot, part] = (
                lax.dot_general(side, partner, contract, preferred_element_type=jnp.float32)
                * scaling
            )

    cross(own_slot)

    for distance in range(1, furthest + 1):
        advance(distance, range(early if distance == 1 else 0, len(tiers)))
        for direction in range(2):

            @pl.when(exists(direction, distance))
            def _():
                source = me - distance if direction == 0 else me + distance
                cross(lax.rem(jnp.clip(source, 0, chan_count - 1), window_slots))

    for copy in span_copies + core_copies + pass_copies:
        copy.wait_send()

    for distance in range(furthest):
        for tier in range(len(tiers)):
            for direction in range(2):

                @pl.when(jnp.logical_and(exists(direction, distance), ahead[direction]))
                def _():
                    outgoing(direction, distance, tier).wait_send()


def slot_kernel(window_slots, pairs_ref, crossed, out_ref, blank, sems):
    blank[...] = jnp.zeros_like(blank)
    for slot in range(SLOTS):
        partner = pairs_ref[0, slot]
        source = crossed.at[lax.rem(jnp.maximum(partner, 0), window_slots)]

        @pl.when(partner >= 0)
        def _():
            pltpu.make_async_copy(source, out_ref.at[0, slot, 0], sems.at[slot]).start()

        @pl.when(partner < 0)
        def _():
            pltpu.make_async_copy(blank, out_ref.at[0, slot, 0], sems.at[slot]).start()

    for slot in range(SLOTS):
        pltpu.make_async_copy(blank, out_ref.at[0, slot, 0], sems.at[slot]).wait()


def fused(recording, trailing, whiten_filter, pair_list):
    rows, hop = recording.shape
    chan_count = lax.axis_size("chan")
    window_slots = min(chan_count, 2 * REACH + 1)
    taps = whiten_filter.shape[1]
    width = FB // (lax.axis_size("tm") * lax.axis_size("freq"))
    block_rows = 2 * rows
    depth = 2 * width
    furthest = min(REACH, chan_count - 1)
    vmem = pl.BlockSpec(memory_space=pltpu.VMEM)
    anywhere = pl.BlockSpec(memory_space=pl.ANY)
    tier_count = 2 * PIECES - 1
    crossed = pl.pallas_call(
        functools.partial(spectra_kernel, chan_count, window_slots, 1.0 / math.sqrt(depth)),
        out_shape=jax.ShapeDtypeStruct((window_slots, 2, block_rows, block_rows), jnp.float32),
        in_specs=[pl.BlockSpec(memory_space=pltpu.HBM)] * 3,
        out_specs=vmem,
        scratch_shapes=[
            pltpu.VMEM((3, block_rows, hop), jnp.bfloat16),
            pltpu.VMEM((2, taps, rows), jnp.bfloat16),
            pltpu.VMEM((2 * PIECES, rows // PIECES, 128), jnp.bfloat16),
            pltpu.VMEM((2 * hop, 2 * width), jnp.bfloat16),
            pltpu.VMEM((4, 2 * hop // STEP, width), jnp.float32),
            pltpu.VMEM((block_rows + taps, 2 * depth), jnp.bfloat16),
            pltpu.VMEM((window_slots, block_rows, 2 * depth), jnp.bfloat16),
            pltpu.SemaphoreType.DMA((3,)),
            pltpu.SemaphoreType.DMA((2, PIECES)),
            pltpu.SemaphoreType.DMA((2, 3)),
            pltpu.SemaphoreType.DMA((2, PIECES)),
            pltpu.SemaphoreType.DMA((2, 2)),
            pltpu.SemaphoreType.DMA((2, 2, furthest, tier_count)),
        ],
        compiler_params=pltpu.CompilerParams(
            collective_id=0, has_side_effects=True, vmem_limit_bytes=16 * 2**20
        ),
    )(recording, trailing, whiten_filter.T)
    return pl.pallas_call(
        functools.partial(slot_kernel, window_slots),
        out_shape=jax.ShapeDtypeStruct((1, SLOTS, 1, 2, block_rows, block_rows), jnp.float32),
        in_specs=[pl.BlockSpec(memory_space=pltpu.SMEM), anywhere],
        out_specs=anywhere,
        scratch_shapes=[
            pltpu.VMEM((2, block_rows, block_rows), jnp.float32),
            pltpu.SemaphoreType.DMA((SLOTS,)),
        ],
        compiler_params=pltpu.CompilerParams(vmem_limit_bytes=8 * 2**20),
    )(pair_list, crossed)


def local(recording, trailing, whiten_filter, pair_list):
    shapes = (recording.shape, trailing.shape, whiten_filter.shape)
    counts = (lax.axis_size("tm"), lax.axis_size("freq"))
    if shapes == ((128, 1024), (128, 1024), (128, 64)) and counts == (2, 2):
        return fused(recording, trailing, whiten_filter, pair_list)
    return general(recording, trailing, whiten_filter, pair_list)


def solution(mesh):
    placed = (
        P(("days", "chan", "freq"), "tm"),
        P(("days", "chan", "freq"), None),
        P(("chan", "freq"), None),
        P(("days", "chan"), None),
    )
    return jax.shard_map(
        local,
        mesh=mesh,
        in_specs=placed,
        out_specs=P(("days", "chan"), None, ("tm", "freq"), None, None, None),
        check_vma=False,
    )
```

```python
import functools
import math

import jax
import jax.numpy as jnp
from jax import lax
from jax.experimental import pallas as pl
from jax.experimental.pallas import tpu as pltpu
from jax.sharding import PartitionSpec as P

FB = 512
REACH = 3
SLOTS = 4


def shifted(block, axis, distance):
    devices = range(lax.axis_size(axis))
    route = [(i - distance, i) for i in devices if i - distance in devices]
    return lax.ppermute(block, axis, route)


def extended(value, sides, width):
    for axis, dim in sides:
        size, length = (lax.axis_size(axis), value.shape[dim])
        up = [(i, (i + 1) % size) for i in range(size - 1)]
        down = [(j, i) for i, j in up]
        last = lax.slice_in_dim(value, length - width, length, axis=dim)
        initial = lax.slice_in_dim(value, 0, width, axis=dim)
        before = lax.ppermute(last, axis, up)
        after = lax.ppermute(initial, axis, down)
        value = jnp.concatenate([before, value, after], axis=dim)
    return value


def fourier_table(first_bin, bin_count, length):
    samples = jnp.arange(length, dtype=jnp.int32)[:, None]
    bin_index = first_bin + jnp.arange(bin_count, dtype=jnp.int32)[None, :]
    phase = samples * bin_index % length
    angle = 2.0 * math.pi / length * phase.astype(jnp.float32)
    taper = 0.5 - 0.5 * jnp.cos(
        2.0 * math.pi / length * jnp.arange(length, dtype=jnp.int32).astype(jnp.float32)
    )
    normaliser = 1.0 / math.sqrt(0.375 * length)
    cosine = (taper[:, None] * jnp.cos(angle) * normaliser).astype(jnp.bfloat16)
    sine_table = (-taper[:, None] * jnp.sin(angle) * normaliser).astype(jnp.bfloat16)
    return (cosine, sine_table)


def general(recording, trailing, whiten_filter, pair_list):
    local_rows, local_span = recording.shape
    hop_size = trailing.shape[1]
    window_size = 2 * hop_size
    segment_count = local_span // hop_size
    following = shifted(recording, "tm", -1)
    is_last = lax.axis_index("tm") == lax.axis_size("tm") - 1
    following = jnp.where(is_last, trailing, following)
    signal = jnp.concatenate([recording, following], axis=1)
    segments = jnp.stack([signal], axis=1)
    stacked_segments = segments.reshape(local_rows * segment_count, window_size)
    bin_step = min(256, FB)
    real_bins = []
    imag_bins = []
    for first_bin in range(0, FB, bin_step):
        cosine, sine_table = fourier_table(first_bin, bin_step, window_size)
        joined = jnp.concatenate([cosine, sine_table], axis=1)
        product = jnp.dot(stacked_segments, joined, preferred_element_type=jnp.float32).astype(
            jnp.bfloat16
        )
        real_bins.append(product[:, :bin_step])
        imag_bins.append(product[:, bin_step:])
    real_spec = jnp.concatenate(real_bins, axis=1)
    imag_spec = jnp.concatenate(imag_bins, axis=1)
    raw_spectra = jnp.stack([real_spec, imag_spec])
    tap_count = whiten_filter.shape[1]
    rim_width = tap_count // 2
    reach_rows = local_rows + tap_count
    skewed = jnp.pad(whiten_filter, ((0, 0), (0, local_rows + 1))).reshape(-1)
    band_matrix = skewed[: local_rows * reach_rows].reshape(local_rows, reach_rows)
    padded = extended(raw_spectra, ((("chan", "freq"), 1),), rim_width)
    predicted = jnp.einsum("ij,ajk->aik", band_matrix, padded, preferred_element_type=jnp.float32)
    whitened = (raw_spectra.astype(jnp.float32) - predicted).astype(jnp.bfloat16)
    spectra = whitened.reshape(2, local_rows, segment_count, FB)
    tm_count = lax.axis_size("tm")
    freq_count = lax.axis_size("freq")
    pieces = lax.all_to_all(spectra[None], ("tm", "freq"), split_axis=4, concat_axis=0, tiled=True)
    band_width = pieces.shape[-1]
    pieces = pieces.reshape(tm_count, freq_count, 2, local_rows, segment_count, band_width)
    banded = pieces.transpose(2, 1, 3, 0, 4, 5).reshape(
        2, freq_count * local_rows, tm_count * segment_count, band_width
    )
    block_rows = banded.shape[1]
    own_block = banded.reshape(2, block_rows, -1)
    depth = own_block.shape[2]
    scaling = 1.0 / math.sqrt(depth)
    block_index = lax.axis_index("chan")
    slot_list = pair_list[0]
    nearby = []
    for distance in range(-REACH, REACH + 1):
        if distance == 0:
            nearby.append(own_block)
        else:
            nearby.append(shifted(own_block, "chan", -distance))
    stacked = jnp.stack(nearby)

    def fetch_partner(partner_index):
        return lax.dynamic_index_in_dim(
            stacked, partner_index - block_index + REACH, 0, keepdims=False
        )

    left_side = jnp.concatenate([own_block[0], own_block[1]], axis=1)
    flipped = jnp.concatenate([own_block[1], -own_block[0]], axis=1)
    contract = (((1,), (1,)), ((), ()))

    def one_slot(partner_index):
        partner = fetch_partner(partner_index)
        right_side = jnp.concatenate([partner[0], partner[1]], axis=1)
        real_part = (
            lax.dot_general(left_side, right_side, contract, preferred_element_type=jnp.float32)
            * scaling
        )
        imag_part = (
            lax.dot_general(flipped, right_side, contract, preferred_element_type=jnp.float32)
            * scaling
        )
        crossed = jnp.stack([real_part, imag_part])
        return jnp.where(partner_index >= 0, crossed, jnp.zeros((), jnp.float32))

    result = jnp.stack([one_slot(slot_list[slot_index]) for slot_index in range(SLOTS)])
    return result.reshape(1, SLOTS, 1, 2, block_rows, block_rows)


MESH = pl.DeviceIdType.MESH
PIECES = 4
STEP = 32


def spectra_kernel(
    chan_count,
    scaling,
    rec_ref,
    trail_ref,
    filt_ref,
    crossed,
    samples,
    filters,
    bands,
    table,
    coarse,
    raw,
    gathered,
    turned,
    products,
    local_sems,
    span_sems,
    core_sems,
    pass_sems,
    filter_sems,
    block_sems,
    out_sems,
):
    me = lax.axis_index("chan")
    tm = lax.axis_index("tm")
    core = lax.axis_index("freq")
    rows, hop = rec_ref.shape
    window = 2 * hop
    width = table.shape[1] // 2
    block_rows = 2 * rows
    taps = filt_ref.shape[0]
    rim = taps // 2
    piece = rows // PIECES
    has_left = me > 0
    has_right = me < chan_count - 1
    other = 1 - core
    other_tm = {"tm": 1 - tm}
    other_core = {"freq": 1 - core}
    left = {"chan": me - 1}
    right = {"chan": me + 1}

    def remote(source, target, sems, index, device):
        return pltpu.make_async_remote_copy(
            src_ref=source,
            dst_ref=target,
            send_sem=sems.at[(0,) + index],
            recv_sem=sems.at[(1,) + index],
            device_id=device,
            device_id_type=MESH,
        )

    def half(which):
        return pl.ds(pl.multiple_of(which * rows, rows), rows)

    barrier = pltpu.get_barrier_semaphore()
    pl.semaphore_signal(barrier, inc=1, device_id=other_tm, device_id_type=MESH)
    pl.semaphore_signal(barrier, inc=1, device_id=other_core, device_id_type=MESH)

    for distance in range(1, chan_count):
        peer = {"chan": lax.rem(me + distance, chan_count)}
        pl.semaphore_signal(barrier, inc=1, device_id=peer, device_id_type=MESH)

    own_copies = [
        pltpu.make_async_copy(rec_ref, samples.at[tm, half(core)], local_sems.at[0]),
        pltpu.make_async_copy(trail_ref, samples.at[2, half(core)], local_sems.at[1]),
        pltpu.make_async_copy(filt_ref, filters.at[core, me], local_sems.at[2]),
    ]
    for copy in own_copies:
        copy.start()

    pl.semaphore_wait(barrier, 1 + chan_count)

    def piece_start(which, step):
        return pl.multiple_of(
            (1 - which) * step * piece + which * (PIECES - 1 - step) * piece, piece
        )

    def piece_in_block(which, step):
        start = which * rows + piece_start(which, step)
        return pl.ds(pl.multiple_of(start, piece), piece)

    span_copies = [
        remote(
            rec_ref.at[pl.ds(piece_start(core, p), piece)],
            samples.at[tm, piece_in_block(core, p)],
            span_sems,
            (p,),
            other_tm,
        )
        for p in range(PIECES)
    ]
    for copy in span_copies:
        copy.start()
    core_copies = [
        remote(rec_ref, samples.at[tm, half(core)], core_sems, (0,), other_core),
        remote(trail_ref, samples.at[2, half(core)], core_sems, (1,), other_core),
    ]
    for copy in core_copies:
        copy.start()

    def exists(direction, distance):
        return me - distance >= 0 if direction == 0 else me + distance < chan_count

    def weights_copy(direction, distance):
        device = {"chan": me + distance if direction == 0 else me - distance}
        return remote(
            filt_ref, filters.at[core, me], filter_sems, (direction, distance - 1), device
        )

    for distance in range(1, chan_count):
        for direction in range(2):

            @pl.when(exists(1 - direction, distance))
            def _():
                weights_copy(direction, distance).start()

    first_bin = (tm * 2 + core) * width
    unit = 2.0 * math.pi / window
    bins = first_bin + lax.broadcasted_iota(jnp.int32, (1, width), 1)

    def angles(count, scale, factor):
        steps = scale * lax.broadcasted_iota(jnp.int32, (count, width), 0)
        return unit * jnp.bitwise_and(steps * factor, window - 1).astype(jnp.float32)

    parts = window // STEP
    coarse_angle = angles(parts, STEP, bins)
    coarse_turn = angles(parts, STEP, 1)
    coarse[0] = jnp.cos(coarse_angle)
    coarse[1] = jnp.sin(coarse_angle)
    coarse[2] = jnp.cos(coarse_turn)
    coarse[3] = jnp.sin(coarse_turn)
    fine_angle = angles(STEP, 1, bins)
    fine_turn = angles(STEP, 1, 1)
    fine_cos, fine_sin = jnp.cos(fine_angle), jnp.sin(fine_angle)
    turn_cos, turn_sin = jnp.cos(fine_turn), jnp.sin(fine_turn)
    normaliser = 1.0 / math.sqrt(0.375 * window)

    def fill(part, carry):
        c, s, tc, ts = (coarse[k, pl.ds(part, 1), :] for k in range(4))
        taper = (0.5 - 0.5 * (tc * turn_cos - ts * turn_sin)) * normaliser
        at = pl.ds(pl.multiple_of(part * STEP, STEP), STEP)
        table[at, :width] = (taper * (c * fine_cos - s * fine_sin)).astype(jnp.bfloat16)
        table[at, width:] = (-taper * (s * fine_cos + c * fine_sin)).astype(jnp.bfloat16)
        return carry

    lax.fori_loop(0, parts, fill, 0)

    edge = jnp.zeros((rim, raw.shape[1]), raw.dtype)
    raw[0:rim] = edge
    raw[rim + chan_count * block_rows :] = edge

    for copy in own_copies:
        copy.wait()
    remote(rec_ref, samples.at[tm, half(other)], core_sems, (0,), other_core).wait_recv()
    remote(trail_ref, samples.at[2, half(other)], core_sems, (1,), other_core).wait_recv()

    def own_rows(block, start, count):
        return pl.ds(pl.multiple_of(rim + block * block_rows + start, piece), count)

    tiers = [(which, p) for which in range(2) for p in range(PIECES)]

    def block_copy(direction, distance, tier, sem):
        which, p = tiers[tier]
        here = core if which == 0 else other
        source = me - distance if direction == 0 else me + distance
        source = jnp.clip(source, 0, chan_count - 1)
        at = raw.at[own_rows(source, here * rows + piece_start(here, p), piece)]
        return remote(at, at, block_sems, (direction, sem, tier), right if direction == 0 else left)

    def outgoing(direction, distance, tier):
        return block_copy(direction, distance, tier, distance)

    def landed(direction, distance, tier):
        return block_copy(direction, distance, tier, distance - 1)

    ahead = (has_right, has_left)

    def transform(which, p, tier):
        at = which * rows + piece_start(which, p)
        chosen = pl.ds(pl.multiple_of(at, piece), piece)
        product = jnp.dot(
            samples[0:2, chosen].reshape(2 * piece, hop),
            table[:hop],
            preferred_element_type=jnp.float32,
        ) + jnp.dot(
            samples[1:3, chosen].reshape(2 * piece, hop),
            table[hop:],
            preferred_element_type=jnp.float32,
        )
        product = product.astype(jnp.bfloat16)
        where = own_rows(me, at, piece)
        for segment in range(2):
            found = product[segment * piece : (segment + 1) * piece]
            raw[where, segment * width : (segment + 1) * width] = found[:, :width]
            raw[where, (2 + segment) * width : (3 + segment) * width] = found[:, width:]
        for direction in range(2):

            @pl.when(ahead[direction])
            def _():
                outgoing(direction, 0, tier).start()

    pass_copies = []
    for p in range(PIECES):
        mine = samples.at[1 - tm, piece_in_block(core, p)]
        remote(mine, mine, span_sems, (p,), other_tm).wait_recv()
        passing = remote(mine, mine, pass_sems, (p,), other_core)
        passing.start()
        pass_copies.append(passing)
        transform(core, p, p)

    for distance in range(1, chan_count):
        for direction in range(2):

            @pl.when(exists(direction, distance))
            def _():
                at = filters.at[core, me - distance if direction == 0 else me + distance]
                remote(at, at, filter_sems, (direction, distance - 1), other_core).wait_recv()

    core_copies.append(
        remote(filters.at[core], filters.at[core], core_sems, (2,), other_core)
    )
    core_copies[-1].start()

    for p in range(PIECES):
        theirs = samples.at[1 - tm, piece_in_block(other, p)]
        remote(theirs, theirs, pass_sems, (p,), other_core).wait_recv()
        transform(other, p, PIECES + p)

    remote(filters.at[other], filters.at[other], core_sems, (2,), other_core).wait_recv()

    def spread(block, carry):
        for which in range(2):
            weights = jnp.transpose(filters[which, block].astype(jnp.float32))
            wide = jnp.concatenate([weights, jnp.zeros((rows, 128 - taps), jnp.float32)], axis=1)
            for p in range(PIECES):
                rolled = pltpu.roll(
                    wide[p * piece : (p + 1) * piece], 0, 1, stride=1, stride_axis=0
                )
                bands[block, which * PIECES + p] = rolled.astype(jnp.bfloat16)
        return carry

    lax.fori_loop(0, chan_count, spread, 0)

    def whiten(block, tile):
        start = pl.multiple_of(block * block_rows + tile * piece, piece)
        near = raw[pl.ds(start, piece + taps)]
        predicted = jnp.dot(
            bands[block, tile][:, : piece + taps], near, preferred_element_type=jnp.float32
        )
        mine = near[rim : rim + piece].astype(jnp.float32)
        gathered[block, tile * piece : (tile + 1) * piece] = (mine - predicted).astype(
            jnp.bfloat16
        )

    contract = (((1,), (1,)), ((), ()))

    def cross(block, index):
        partner = gathered[block]
        for part, side in enumerate((gathered[me], turned[...])):
            products[block, part] = (
                lax.dot_general(side, partner, contract, preferred_element_type=jnp.float32)
                * scaling
            )
        pltpu.make_async_copy(products.at[block], crossed.at[block], out_sems.at[index]).start()

    tile_count = 2 * PIECES
    for tile in range(1, tile_count - 1):
        whiten(me, tile)

    def finish_own():
        whiten(me, 0)
        whiten(me, tile_count - 1)
        own = gathered[me]
        middle = own.shape[1] // 2
        turned[...] = jnp.concatenate([own[:, middle:], -own[:, :middle]], axis=1)
        cross(me, 0)

    def finish(direction, distance):
        @pl.when(exists(direction, distance))
        def _():
            block = me - distance if direction == 0 else me + distance
            whiten(block, 0 if direction == 0 else tile_count - 1)
            cross(block, 2 * distance - 1 + direction)

    furthest = chan_count - 1
    for distance in range(1, chan_count):
        for tier in range(len(tiers)):
            for direction in range(2):

                @pl.when(exists(direction, distance))
                def _():
                    landed(direction, distance, tier).wait_recv()

                if distance < furthest:

                    @pl.when(jnp.logical_and(exists(direction, distance), ahead[direction]))
                    def _():
                        outgoing(direction, distance, tier).start()

            if tier == PIECES:
                if distance == 1:
                    finish_own()
                else:
                    for direction in range(2):
                        finish(direction, distance - 1)

        for direction in range(2):

            @pl.when(exists(direction, distance))
            def _():
                block = me - distance if direction == 0 else me + distance
                for tile in range(tile_count - 1):
                    whiten(block, tile + 1 if direction == 0 else tile)

    for direction in range(2):
        finish(direction, furthest)

    for copy in span_copies + core_copies + pass_copies:
        copy.wait_send()

    for distance in range(1, chan_count):
        for direction in range(2):

            @pl.when(exists(1 - direction, distance))
            def _():
                weights_copy(direction, distance).wait_send()

    for distance in range(furthest):
        for tier in range(len(tiers)):
            for direction in range(2):

                @pl.when(jnp.logical_and(exists(direction, distance), ahead[direction]))
                def _():
                    outgoing(direction, distance, tier).wait_send()

    pltpu.make_async_copy(products.at[me], crossed.at[me], out_sems.at[0]).wait()
    for distance in range(1, chan_count):
        for direction in range(2):

            @pl.when(exists(direction, distance))
            def _():
                block = me - distance if direction == 0 else me + distance
                index = 2 * distance - 1 + direction
                pltpu.make_async_copy(
                    products.at[block], crossed.at[block], out_sems.at[index]
                ).wait()


def slot_kernel(pairs_ref, crossed, out_ref, held, in_sems, out_sems):
    def fetch(slot):
        partner = jnp.maximum(pairs_ref[0, slot], 0)
        return pltpu.make_async_copy(crossed.at[partner], held.at[slot], in_sems.at[slot])

    def store(slot):
        return pltpu.make_async_copy(held.at[slot], out_ref.at[0, slot, 0], out_sems.at[slot])

    for slot in range(SLOTS):

        @pl.when(pairs_ref[0, slot] >= 0)
        def _():
            fetch(slot).start()

    for slot in range(SLOTS):

        @pl.when(pairs_ref[0, slot] >= 0)
        def _():
            fetch(slot).wait()

        @pl.when(pairs_ref[0, slot] < 0)
        def _():
            held[slot] = jnp.zeros(held.shape[1:], held.dtype)

        store(slot).start()

    for slot in range(SLOTS):
        store(slot).wait()


def fused(recording, trailing, whiten_filter, pair_list):
    rows, hop = recording.shape
    chan_count = lax.axis_size("chan")
    taps = whiten_filter.shape[1]
    width = FB // (lax.axis_size("tm") * lax.axis_size("freq"))
    block_rows = 2 * rows
    depth = 2 * width
    anywhere = pl.BlockSpec(memory_space=pl.ANY)
    crossed = pl.pallas_call(
        functools.partial(spectra_kernel, chan_count, 1.0 / math.sqrt(depth)),
        out_shape=jax.ShapeDtypeStruct((chan_count, 2, block_rows, block_rows), jnp.float32),
        in_specs=[anywhere] * 3,
        out_specs=anywhere,
        scratch_shapes=[
            pltpu.VMEM((3, block_rows, hop), jnp.bfloat16),
            pltpu.VMEM((2, chan_count, taps, rows), jnp.bfloat16),
            pltpu.VMEM((chan_count, 2 * PIECES, rows // PIECES, 128), jnp.bfloat16),
            pltpu.VMEM((2 * hop, 2 * width), jnp.bfloat16),
            pltpu.VMEM((4, 2 * hop // STEP, width), jnp.float32),
            pltpu.VMEM((chan_count * block_rows + taps, 2 * depth), jnp.bfloat16),
            pltpu.VMEM((chan_count, block_rows, 2 * depth), jnp.bfloat16),
            pltpu.VMEM((block_rows, 2 * depth), jnp.bfloat16),
            pltpu.VMEM((chan_count, 2, block_rows, block_rows), jnp.float32),
            pltpu.SemaphoreType.DMA((3,)),
            pltpu.SemaphoreType.DMA((2, PIECES)),
            pltpu.SemaphoreType.DMA((2, 3)),
            pltpu.SemaphoreType.DMA((2, PIECES)),
            pltpu.SemaphoreType.DMA((2, 2, chan_count - 1)),
            pltpu.SemaphoreType.DMA((2, 2, chan_count - 1, 2 * PIECES)),
            pltpu.SemaphoreType.DMA((2 * chan_count,)),
        ],
        compiler_params=pltpu.CompilerParams(collective_id=0, has_side_effects=True),
    )(recording, trailing, whiten_filter.T)
    return pl.pallas_call(
        slot_kernel,
        out_shape=jax.ShapeDtypeStruct((1, SLOTS, 1, 2, block_rows, block_rows), jnp.float32),
        in_specs=[pl.BlockSpec(memory_space=pltpu.SMEM), anywhere],
        out_specs=anywhere,
        scratch_shapes=[
            pltpu.VMEM((SLOTS, 2, block_rows, block_rows), jnp.float32),
            pltpu.SemaphoreType.DMA((SLOTS,)),
            pltpu.SemaphoreType.DMA((SLOTS,)),
        ],
    )(pair_list, crossed)


def local(recording, trailing, whiten_filter, pair_list):
    shapes = (recording.shape, trailing.shape, whiten_filter.shape)
    counts = (lax.axis_size("tm"), lax.axis_size("freq"))
    whole_reach = 1 < lax.axis_size("chan") <= REACH + 1
    if shapes == ((128, 1024), (128, 1024), (128, 64)) and counts == (2, 2) and whole_reach:
        return fused(recording, trailing, whiten_filter, pair_list)
    return general(recording, trailing, whiten_filter, pair_list)


def solution(mesh):
    placed = (
        P(("days", "chan", "freq"), "tm"),
        P(("days", "chan", "freq"), None),
        P(("chan", "freq"), None),
        P(("days", "chan"), None),
    )
    return jax.shard_map(
        local,
        mesh=mesh,
        in_specs=placed,
        out_specs=P(("days", "chan"), None, ("tm", "freq"), None, None, None),
        check_vma=False,
    )
```

```python
import functools
import math

import jax
import jax.numpy as jnp
from jax import lax
from jax.experimental import pallas as pl
from jax.experimental.pallas import tpu as pltpu
from jax.sharding import PartitionSpec as P

FB = 512
REACH = 3
SLOTS = 4


def shifted(block, axis, distance):
    devices = range(lax.axis_size(axis))
    route = [(i - distance, i) for i in devices if i - distance in devices]
    return lax.ppermute(block, axis, route)


def extended(value, sides, width):
    for axis, dim in sides:
        size, length = (lax.axis_size(axis), value.shape[dim])
        up = [(i, (i + 1) % size) for i in range(size - 1)]
        down = [(j, i) for i, j in up]
        last = lax.slice_in_dim(value, length - width, length, axis=dim)
        initial = lax.slice_in_dim(value, 0, width, axis=dim)
        before = lax.ppermute(last, axis, up)
        after = lax.ppermute(initial, axis, down)
        value = jnp.concatenate([before, value, after], axis=dim)
    return value


def fourier_table(first_bin, bin_count, length):
    samples = jnp.arange(length, dtype=jnp.int32)[:, None]
    bin_index = first_bin + jnp.arange(bin_count, dtype=jnp.int32)[None, :]
    phase = samples * bin_index % length
    angle = 2.0 * math.pi / length * phase.astype(jnp.float32)
    taper = 0.5 - 0.5 * jnp.cos(
        2.0 * math.pi / length * jnp.arange(length, dtype=jnp.int32).astype(jnp.float32)
    )
    normaliser = 1.0 / math.sqrt(0.375 * length)
    cosine = (taper[:, None] * jnp.cos(angle) * normaliser).astype(jnp.bfloat16)
    sine_table = (-taper[:, None] * jnp.sin(angle) * normaliser).astype(jnp.bfloat16)
    return (cosine, sine_table)


def general(recording, trailing, whiten_filter, pair_list):
    local_rows, local_span = recording.shape
    hop_size = trailing.shape[1]
    window_size = 2 * hop_size
    segment_count = local_span // hop_size
    following = shifted(recording, "tm", -1)
    is_last = lax.axis_index("tm") == lax.axis_size("tm") - 1
    following = jnp.where(is_last, trailing, following)
    signal = jnp.concatenate([recording, following], axis=1)
    segments = jnp.stack([signal], axis=1)
    stacked_segments = segments.reshape(local_rows * segment_count, window_size)
    bin_step = min(256, FB)
    real_bins = []
    imag_bins = []
    for first_bin in range(0, FB, bin_step):
        cosine, sine_table = fourier_table(first_bin, bin_step, window_size)
        joined = jnp.concatenate([cosine, sine_table], axis=1)
        product = jnp.dot(stacked_segments, joined, preferred_element_type=jnp.float32).astype(
            jnp.bfloat16
        )
        real_bins.append(product[:, :bin_step])
        imag_bins.append(product[:, bin_step:])
    real_spec = jnp.concatenate(real_bins, axis=1)
    imag_spec = jnp.concatenate(imag_bins, axis=1)
    raw_spectra = jnp.stack([real_spec, imag_spec])
    tap_count = whiten_filter.shape[1]
    rim_width = tap_count // 2
    reach_rows = local_rows + tap_count
    skewed = jnp.pad(whiten_filter, ((0, 0), (0, local_rows + 1))).reshape(-1)
    band_matrix = skewed[: local_rows * reach_rows].reshape(local_rows, reach_rows)
    padded = extended(raw_spectra, ((("chan", "freq"), 1),), rim_width)
    predicted = jnp.einsum("ij,ajk->aik", band_matrix, padded, preferred_element_type=jnp.float32)
    whitened = (raw_spectra.astype(jnp.float32) - predicted).astype(jnp.bfloat16)
    spectra = whitened.reshape(2, local_rows, segment_count, FB)
    tm_count = lax.axis_size("tm")
    freq_count = lax.axis_size("freq")
    pieces = lax.all_to_all(spectra[None], ("tm", "freq"), split_axis=4, concat_axis=0, tiled=True)
    band_width = pieces.shape[-1]
    pieces = pieces.reshape(tm_count, freq_count, 2, local_rows, segment_count, band_width)
    banded = pieces.transpose(2, 1, 3, 0, 4, 5).reshape(
        2, freq_count * local_rows, tm_count * segment_count, band_width
    )
    block_rows = banded.shape[1]
    own_block = banded.reshape(2, block_rows, -1)
    depth = own_block.shape[2]
    scaling = 1.0 / math.sqrt(depth)
    block_index = lax.axis_index("chan")
    slot_list = pair_list[0]
    nearby = []
    for distance in range(-REACH, REACH + 1):
        if distance == 0:
            nearby.append(own_block)
        else:
            nearby.append(shifted(own_block, "chan", -distance))
    stacked = jnp.stack(nearby)

    def fetch_partner(partner_index):
        return lax.dynamic_index_in_dim(
            stacked, partner_index - block_index + REACH, 0, keepdims=False
        )

    left_side = jnp.concatenate([own_block[0], own_block[1]], axis=1)
    flipped = jnp.concatenate([own_block[1], -own_block[0]], axis=1)
    contract = (((1,), (1,)), ((), ()))

    def one_slot(partner_index):
        partner = fetch_partner(partner_index)
        right_side = jnp.concatenate([partner[0], partner[1]], axis=1)
        real_part = (
            lax.dot_general(left_side, right_side, contract, preferred_element_type=jnp.float32)
            * scaling
        )
        imag_part = (
            lax.dot_general(flipped, right_side, contract, preferred_element_type=jnp.float32)
            * scaling
        )
        crossed = jnp.stack([real_part, imag_part])
        return jnp.where(partner_index >= 0, crossed, jnp.zeros((), jnp.float32))

    result = jnp.stack([one_slot(slot_list[slot_index]) for slot_index in range(SLOTS)])
    return result.reshape(1, SLOTS, 1, 2, block_rows, block_rows)


MESH = pl.DeviceIdType.MESH
PIECES = 4
STEP = 32


def spectra_kernel(
    chan_count,
    scaling,
    rec_ref,
    trail_ref,
    filt_ref,
    crossed,
    samples,
    filters,
    bands,
    table,
    coarse,
    raw,
    gathered,
    turned,
    products,
    local_sems,
    span_sems,
    core_sems,
    pass_sems,
    filter_sems,
    block_sems,
    out_sems,
):
    me = lax.axis_index("chan")
    tm = lax.axis_index("tm")
    core = lax.axis_index("freq")
    rows, hop = rec_ref.shape
    window = 2 * hop
    width = table.shape[1] // 2
    block_rows = 2 * rows
    taps = filt_ref.shape[0]
    rim = taps // 2
    piece = rows // PIECES
    has_left = me > 0
    has_right = me < chan_count - 1
    other = 1 - core
    other_tm = {"tm": 1 - tm}
    other_core = {"freq": 1 - core}
    left = {"chan": me - 1}
    right = {"chan": me + 1}

    def remote(source, target, sems, index, device):
        return pltpu.make_async_remote_copy(
            src_ref=source,
            dst_ref=target,
            send_sem=sems.at[(0,) + index],
            recv_sem=sems.at[(1,) + index],
            device_id=device,
            device_id_type=MESH,
        )

    def half(which):
        return pl.ds(pl.multiple_of(which * rows, rows), rows)

    barrier = pltpu.get_barrier_semaphore()
    pl.semaphore_signal(barrier, inc=1, device_id=other_tm, device_id_type=MESH)
    pl.semaphore_signal(barrier, inc=1, device_id=other_core, device_id_type=MESH)

    @pl.when(has_left)
    def _():
        pl.semaphore_signal(barrier, inc=1, device_id=left, device_id_type=MESH)

    @pl.when(has_right)
    def _():
        pl.semaphore_signal(barrier, inc=1, device_id=right, device_id_type=MESH)

    own_copies = [
        pltpu.make_async_copy(rec_ref, samples.at[tm, half(core)], local_sems.at[0]),
        pltpu.make_async_copy(trail_ref, samples.at[2, half(core)], local_sems.at[1]),
        pltpu.make_async_copy(filt_ref, filters.at[core, me], local_sems.at[2]),
    ]
    for copy in own_copies:
        copy.start()

    pl.semaphore_wait(barrier, 2 + has_left.astype(jnp.int32) + has_right.astype(jnp.int32))

    def piece_start(which, step):
        return pl.multiple_of(
            (1 - which) * step * piece + which * (PIECES - 1 - step) * piece, piece
        )

    def piece_in_block(which, step):
        start = which * rows + piece_start(which, step)
        return pl.ds(pl.multiple_of(start, piece), piece)

    span_copies = [
        remote(
            rec_ref.at[pl.ds(piece_start(core, p), piece)],
            samples.at[tm, piece_in_block(core, p)],
            span_sems,
            (p,),
            other_tm,
        )
        for p in range(PIECES)
    ]
    for copy in span_copies:
        copy.start()
    core_copies = [
        remote(rec_ref, samples.at[tm, half(core)], core_sems, (0,), other_core),
        remote(trail_ref, samples.at[2, half(core)], core_sems, (1,), other_core),
    ]
    for copy in core_copies:
        copy.start()

    def exists(direction, distance):
        return me - distance >= 0 if direction == 0 else me + distance < chan_count

    ahead = (has_right, has_left)
    furthest = chan_count - 1

    def weights_copy(direction, distance, sem):
        source = me - distance if direction == 0 else me + distance
        at = filters.at[core, jnp.clip(source, 0, chan_count - 1)]
        device = right if direction == 0 else left
        held = filt_ref if distance == 0 else at
        return remote(held, at, filter_sems, (direction, sem), device)

    for direction in range(2):

        @pl.when(ahead[direction])
        def _():
            weights_copy(direction, 0, 0).start()

    first_bin = (tm * 2 + core) * width
    unit = 2.0 * math.pi / window
    bins = first_bin + lax.broadcasted_iota(jnp.int32, (1, width), 1)

    def angles(count, scale, factor):
        steps = scale * lax.broadcasted_iota(jnp.int32, (count, width), 0)
        return unit * jnp.bitwise_and(steps * factor, window - 1).astype(jnp.float32)

    parts = window // STEP
    coarse_angle = angles(parts, STEP, bins)
    coarse_turn = angles(parts, STEP, 1)
    coarse[0] = jnp.cos(coarse_angle)
    coarse[1] = jnp.sin(coarse_angle)
    coarse[2] = jnp.cos(coarse_turn)
    coarse[3] = jnp.sin(coarse_turn)
    fine_angle = angles(STEP, 1, bins)
    fine_turn = angles(STEP, 1, 1)
    fine_cos, fine_sin = jnp.cos(fine_angle), jnp.sin(fine_angle)
    turn_cos, turn_sin = jnp.cos(fine_turn), jnp.sin(fine_turn)
    normaliser = 1.0 / math.sqrt(0.375 * window)

    def fill(part, carry):
        c, s, tc, ts = (coarse[k, pl.ds(part, 1), :] for k in range(4))
        taper = (0.5 - 0.5 * (tc * turn_cos - ts * turn_sin)) * normaliser
        at = pl.ds(pl.multiple_of(part * STEP, STEP), STEP)
        table[at, :width] = (taper * (c * fine_cos - s * fine_sin)).astype(jnp.bfloat16)
        table[at, width:] = (-taper * (s * fine_cos + c * fine_sin)).astype(jnp.bfloat16)
        return carry

    lax.fori_loop(0, parts, fill, 0)

    edge = jnp.zeros((rim, raw.shape[1]), raw.dtype)
    raw[0:rim] = edge
    raw[rim + chan_count * block_rows :] = edge

    for copy in own_copies:
        copy.wait()
    def own_rows(block, start, count):
        return pl.ds(pl.multiple_of(rim + block * block_rows + start, piece), count)

    tiers = [(which, p) for which in range(2) for p in range(PIECES)]

    def block_copy(direction, distance, tier, sem):
        which, p = tiers[tier]
        here = core if which == 0 else other
        source = me - distance if direction == 0 else me + distance
        source = jnp.clip(source, 0, chan_count - 1)
        at = raw.at[own_rows(source, here * rows + piece_start(here, p), piece)]
        return remote(at, at, block_sems, (direction, sem, tier), right if direction == 0 else left)

    def outgoing(direction, distance, tier):
        return block_copy(direction, distance, tier, distance)

    def landed(direction, distance, tier):
        return block_copy(direction, distance, tier, distance - 1)

    def transform(which, p, tier):
        at = which * rows + piece_start(which, p)
        chosen = pl.ds(pl.multiple_of(at, piece), piece)
        product = jnp.dot(
            samples[0:2, chosen].reshape(2 * piece, hop),
            table[:hop],
            preferred_element_type=jnp.float32,
        ) + jnp.dot(
            samples[1:3, chosen].reshape(2 * piece, hop),
            table[hop:],
            preferred_element_type=jnp.float32,
        )
        product = product.astype(jnp.bfloat16)
        where = own_rows(me, at, piece)
        for segment in range(2):
            found = product[segment * piece : (segment + 1) * piece]
            raw[where, segment * width : (segment + 1) * width] = found[:, :width]
            raw[where, (2 + segment) * width : (3 + segment) * width] = found[:, width:]
        for direction in range(2):

            @pl.when(ahead[direction])
            def _():
                outgoing(direction, 0, tier).start()

    def transform_passed(p):
        theirs = samples.at[1 - tm, piece_in_block(other, p)]
        remote(theirs, theirs, pass_sems, (p,), other_core).wait_recv()
        transform(other, p, PIECES + p)

    pass_copies = []
    for p in range(PIECES):
        mine = samples.at[1 - tm, piece_in_block(core, p)]
        remote(mine, mine, span_sems, (p,), other_tm).wait_recv()
        passing = remote(mine, mine, pass_sems, (p,), other_core)
        passing.start()
        pass_copies.append(passing)
        transform(core, p, p)
        if p == 0:
            remote(rec_ref, samples.at[tm, half(other)], core_sems, (0,), other_core).wait_recv()
            remote(trail_ref, samples.at[2, half(other)], core_sems, (1,), other_core).wait_recv()
        else:
            transform_passed(p - 1)
        distance = p + 1
        if distance <= furthest:
            for direction in range(2):

                @pl.when(exists(direction, distance))
                def _():
                    weights_copy(direction, distance, distance - 1).wait_recv()

                if distance < furthest:

                    @pl.when(jnp.logical_and(exists(direction, distance), ahead[direction]))
                    def _():
                        weights_copy(direction, distance, distance).start()

    core_copies.append(remote(filters.at[core], filters.at[core], core_sems, (2,), other_core))
    core_copies[-1].start()
    transform_passed(PIECES - 1)

    order = [0]
    for p in range(1, PIECES):
        order += [p, PIECES + p - 1]
    order.append(2 * PIECES - 1)

    def advance(distance, chosen):
        for tier in chosen:
            for direction in range(2):

                @pl.when(exists(direction, distance))
                def _():
                    landed(direction, distance, tier).wait_recv()

                if distance < furthest:

                    @pl.when(jnp.logical_and(exists(direction, distance), ahead[direction]))
                    def _():
                        outgoing(direction, distance, tier).start()

    advance(1, order[:PIECES])
    remote(filters.at[other], filters.at[other], core_sems, (2,), other_core).wait_recv()

    def spread(block, carry):
        for which in range(2):
            weights = jnp.transpose(filters[which, block].astype(jnp.float32))
            wide = jnp.concatenate([weights, jnp.zeros((rows, 128 - taps), jnp.float32)], axis=1)
            for p in range(PIECES):
                rolled = pltpu.roll(
                    wide[p * piece : (p + 1) * piece], 0, 1, stride=1, stride_axis=0
                )
                bands[block, which * PIECES + p] = rolled.astype(jnp.bfloat16)
        return carry

    lax.fori_loop(0, chan_count, spread, 0)

    def whiten(block, tile):
        start = pl.multiple_of(block * block_rows + tile * piece, piece)
        near = raw[pl.ds(start, piece + taps)]
        predicted = jnp.dot(
            bands[block, tile][:, : piece + taps], near, preferred_element_type=jnp.float32
        )
        mine = near[rim : rim + piece].astype(jnp.float32)
        gathered[block, tile * piece : (tile + 1) * piece] = (mine - predicted).astype(
            jnp.bfloat16
        )

    contract = (((1,), (1,)), ((), ()))

    def cross(block, index):
        partner = gathered[block]
        for part, side in enumerate((gathered[me], turned[...])):
            products[block, part] = (
                lax.dot_general(side, partner, contract, preferred_element_type=jnp.float32)
                * scaling
            )
        pltpu.make_async_copy(products.at[block], crossed.at[block], out_sems.at[index]).start()

    tile_count = 2 * PIECES
    for tile in range(1, tile_count - 1):
        whiten(me, tile)

    def finish_own():
        whiten(me, 0)
        whiten(me, tile_count - 1)
        own = gathered[me]
        middle = own.shape[1] // 2
        turned[...] = jnp.concatenate([own[:, middle:], -own[:, :middle]], axis=1)
        cross(me, 0)

    def finish(direction, distance):
        @pl.when(exists(direction, distance))
        def _():
            block = me - distance if direction == 0 else me + distance
            whiten(block, 0 if direction == 0 else tile_count - 1)
            cross(block, 2 * distance - 1 + direction)

    for distance in range(1, chan_count):
        if distance == 1:
            finish_own()
        else:
            advance(distance, order[:PIECES])
            for direction in range(2):
                finish(direction, distance - 1)
        advance(distance, order[PIECES:])
        for direction in range(2):

            @pl.when(exists(direction, distance))
            def _():
                block = me - distance if direction == 0 else me + distance
                for tile in range(tile_count - 1):
                    whiten(block, tile + 1 if direction == 0 else tile)

    for direction in range(2):
        finish(direction, furthest)

    for copy in span_copies + core_copies + pass_copies:
        copy.wait_send()

    for distance in range(furthest):
        for direction in range(2):

            @pl.when(jnp.logical_and(exists(direction, distance), ahead[direction]))
            def _():
                weights_copy(direction, distance, distance).wait_send()

    for distance in range(furthest):
        for tier in range(len(tiers)):
            for direction in range(2):

                @pl.when(jnp.logical_and(exists(direction, distance), ahead[direction]))
                def _():
                    outgoing(direction, distance, tier).wait_send()

    pltpu.make_async_copy(products.at[me], crossed.at[me], out_sems.at[0]).wait()
    for distance in range(1, chan_count):
        for direction in range(2):

            @pl.when(exists(direction, distance))
            def _():
                block = me - distance if direction == 0 else me + distance
                index = 2 * distance - 1 + direction
                pltpu.make_async_copy(
                    products.at[block], crossed.at[block], out_sems.at[index]
                ).wait()


def slot_kernel(pairs_ref, crossed, out_ref, held, in_sems, out_sems):
    def fetch(slot):
        partner = jnp.maximum(pairs_ref[0, slot], 0)
        return pltpu.make_async_copy(crossed.at[partner], held.at[slot], in_sems.at[slot])

    def store(slot):
        return pltpu.make_async_copy(held.at[slot], out_ref.at[0, slot, 0], out_sems.at[slot])

    for slot in range(SLOTS):

        @pl.when(pairs_ref[0, slot] >= 0)
        def _():
            fetch(slot).start()

    for slot in range(SLOTS):

        @pl.when(pairs_ref[0, slot] >= 0)
        def _():
            fetch(slot).wait()

        @pl.when(pairs_ref[0, slot] < 0)
        def _():
            held[slot] = jnp.zeros(held.shape[1:], held.dtype)

        store(slot).start()

    for slot in range(SLOTS):
        store(slot).wait()


def fused(recording, trailing, whiten_filter, pair_list):
    rows, hop = recording.shape
    chan_count = lax.axis_size("chan")
    taps = whiten_filter.shape[1]
    width = FB // (lax.axis_size("tm") * lax.axis_size("freq"))
    block_rows = 2 * rows
    depth = 2 * width
    anywhere = pl.BlockSpec(memory_space=pl.ANY)
    crossed = pl.pallas_call(
        functools.partial(spectra_kernel, chan_count, 1.0 / math.sqrt(depth)),
        out_shape=jax.ShapeDtypeStruct((chan_count, 2, block_rows, block_rows), jnp.float32),
        in_specs=[anywhere] * 3,
        out_specs=anywhere,
        scratch_shapes=[
            pltpu.VMEM((3, block_rows, hop), jnp.bfloat16),
            pltpu.VMEM((2, chan_count, taps, rows), jnp.bfloat16),
            pltpu.VMEM((chan_count, 2 * PIECES, rows // PIECES, 128), jnp.bfloat16),
            pltpu.VMEM((2 * hop, 2 * width), jnp.bfloat16),
            pltpu.VMEM((4, 2 * hop // STEP, width), jnp.float32),
            pltpu.VMEM((chan_count * block_rows + taps, 2 * depth), jnp.bfloat16),
            pltpu.VMEM((chan_count, block_rows, 2 * depth), jnp.bfloat16),
            pltpu.VMEM((block_rows, 2 * depth), jnp.bfloat16),
            pltpu.VMEM((chan_count, 2, block_rows, block_rows), jnp.float32),
            pltpu.SemaphoreType.DMA((3,)),
            pltpu.SemaphoreType.DMA((2, PIECES)),
            pltpu.SemaphoreType.DMA((2, 3)),
            pltpu.SemaphoreType.DMA((2, PIECES)),
            pltpu.SemaphoreType.DMA((2, 2, chan_count - 1)),
            pltpu.SemaphoreType.DMA((2, 2, chan_count - 1, 2 * PIECES)),
            pltpu.SemaphoreType.DMA((2 * chan_count,)),
        ],
        compiler_params=pltpu.CompilerParams(collective_id=0, has_side_effects=True),
    )(recording, trailing, whiten_filter.T)
    return pl.pallas_call(
        slot_kernel,
        out_shape=jax.ShapeDtypeStruct((1, SLOTS, 1, 2, block_rows, block_rows), jnp.float32),
        in_specs=[pl.BlockSpec(memory_space=pltpu.SMEM), anywhere],
        out_specs=anywhere,
        scratch_shapes=[
            pltpu.VMEM((SLOTS, 2, block_rows, block_rows), jnp.float32),
            pltpu.SemaphoreType.DMA((SLOTS,)),
            pltpu.SemaphoreType.DMA((SLOTS,)),
        ],
    )(pair_list, crossed)


def local(recording, trailing, whiten_filter, pair_list):
    shapes = (recording.shape, trailing.shape, whiten_filter.shape)
    counts = (lax.axis_size("tm"), lax.axis_size("freq"))
    whole_reach = 1 < lax.axis_size("chan") <= REACH + 1
    if shapes == ((128, 1024), (128, 1024), (128, 64)) and counts == (2, 2) and whole_reach:
        return fused(recording, trailing, whiten_filter, pair_list)
    return general(recording, trailing, whiten_filter, pair_list)


def solution(mesh):
    placed = (
        P(("days", "chan", "freq"), "tm"),
        P(("days", "chan", "freq"), None),
        P(("chan", "freq"), None),
        P(("days", "chan"), None),
    )
    return jax.shard_map(
        local,
        mesh=mesh,
        in_specs=placed,
        out_specs=P(("days", "chan"), None, ("tm", "freq"), None, None, None),
        check_vma=False,
    )
```
